128 devices in a mesh: space: 32 (over x, y, z_hi), shot: 4 (over z_lo, core).
Axes of the slice: x: 4, y: 4, z: 4 (z_hi: 2, z_lo: 2; z = z_hi * 2 + z_lo), core: 2. Of those that a mesh axis runs over, the one named last changes fastest.
Arguments:
- adjoint_state: float32 [4, 9, 128, 128, 256], P('shot', None, 'space'), may hold values from -6 to 6
- forward_strain: bfloat16 [4, 4, 6, 128, 128, 256], P('shot', None, None, 'space'), may hold values from -6 to 6
- traces: float32 [4, 4, 256], P('shot'), may hold values from -12 to 12
- receivers: int32 [4, 256], P('shot'), may hold values from 0 to 4194303
- sections: int32 [32], replicated, may hold values from 0 to 1
- lame_lambda: float32 [128, 128, 256], P('space'), may hold values from 1 to 2
- lame_mu: float32 [128, 128, 256], P('space'), may hold values from 0.3 to 1
- buoyancy: float32 [128, 128, 256], P('space'), may hold values from 0.5 to 1
Outputs:
- final_state: float32 [4, 9, 128, 128, 256], P('shot', None, 'space')
- model_new: float32 [2, 128, 128, 256], P(None, 'space')
The draws below stay inside these ranges and needn't reach their ends.
Inputs may be any that keep to these rules, and one draw needn't show every extreme that they name: `sections`: 0 marks a water slab, 1 a solid one. A receiver's flat cell index is x * 128 * 256 + y * 256 + z; several receivers may share a cell.
All inputs are finite; a program needn't handle non-finite values. Where the reference program divides by a largest or mean magnitude, that divisor is 1e-20 or more.
Results may differ from the reference program's by a relative error of at most 0.0003.
Values sent between devices are 32-bit elements; how exact they have to be, the bound alone decides.
No kernel may reach another device: no remote copies, remote signals or barrier semaphores. Data moves between devices by JAX's collectives and lax.ppermute only.
A program may use at most 128 MiB of HBM per device.

```python
import jax
import jax.numpy as jnp
from jax import lax

CX = 4
NY = 128
NZ = 256
STEPS = 4
RECS = 256
SHOTS = 4
SLABS = 32
NX = 128


def plant(array, key, smallest, high):
    index_at = [jax.random.randint(jax.random.fold_in(key, axis), (), 0, length) for axis, length in enumerate(array.shape)]
    main_axis = array.shape.index(max(array.shape))
    next_to = index_at[:main_axis] + [(index_at[main_axis] + 1) % array.shape[main_axis]] + index_at[main_axis + 1:]
    return array.at[tuple(index_at)].set(smallest).at[tuple(next_to)].set(high)


def steps_of(key, extent, split, least, top_value):
    def one(position, shards_of):
        steps = jax.random.uniform(jax.random.fold_in(jax.random.fold_in(key, 6), position), (shards_of,), jnp.float32, least / len(split), top_value / len(split))
        return jnp.repeat(jnp.exp(steps), extent[position] // shards_of).reshape((-1,) + (1,) * (len(extent) - position - 1))

    gain = one(*split[0])
    for cut in split[1:]:
        gain = gain * one(*cut)
    return gain


def noise(own_key, extent, scale, most, cuts=(), kind=jnp.bfloat16):
    factor_of = steps_of(own_key, extent, cuts, -0.22, 0.18) if cuts else 1.0
    result = jax.random.normal(own_key, extent, jnp.float32) * scale * factor_of
    return jnp.minimum(jnp.maximum(result, -most), most).astype(kind)


def setup_inputs(seed: int = 0) -> dict:
    keys = jax.random.split(jax.random.key(seed), 9)
    return {
        "adjoint_state": noise(keys[0], (SHOTS, 9, NX, NY, NZ), 1.0, 6.0, ((0, 4), (2, 32)), jnp.float32),
        "forward_strain": noise(keys[1], (SHOTS, STEPS, 6, NX, NY, NZ), 1.0, 6.0, ((0, 4), (3, 32))),
        "traces": noise(keys[2], (SHOTS, STEPS, RECS), 3.0, 12.0, ((0, 4),), jnp.float32),
        "receivers": plant(jax.random.randint(keys[3], (SHOTS, RECS), 0, NX * NY * NZ), jax.random.fold_in(keys[3], 1), 0, (NX * NY * NZ) - 1).astype(jnp.int32),
        "sections": plant(jax.random.randint(keys[4], (SLABS,), 0, 2), jax.random.fold_in(keys[4], 1), 0, 1).astype(jnp.int32),
        "lame_lambda": jnp.clip(1.0 + 1.0 * jax.random.uniform(keys[5], (NX, NY, NZ), jnp.float32) ** steps_of(keys[5], (NX, NY, NZ), ((0, 32),), -0.2, 0.2), 1.0, 2.0),
        "lame_mu": jnp.clip(0.3 + 0.7 * jax.random.uniform(keys[6], (NX, NY, NZ), jnp.float32) ** steps_of(keys[6], (NX, NY, NZ), ((0, 32),), -0.2, 0.2), 0.3, 1.0),
        "buoyancy": jnp.clip(0.5 + 0.5 * jax.random.uniform(keys[7], (NX, NY, NZ), jnp.float32) ** steps_of(keys[7], (NX, NY, NZ), ((0, 32),), -0.2, 0.2), 0.5, 1.0),
    }


COURANT = 0.15
RATE = 0.2
EPS = 1e-6


def back_diff(field, axis):
    count = field.shape[axis]
    earlier = jnp.concatenate([jnp.zeros_like(lax.slice_in_dim(field, 0, 1, axis=axis)), lax.slice_in_dim(field, 0, count - 1, axis=axis)], axis=axis)
    return field - earlier


def fore_diff(field, axis):
    count = field.shape[axis]
    later = jnp.concatenate([lax.slice_in_dim(field, 1, count, axis=axis), jnp.zeros_like(lax.slice_in_dim(field, 0, 1, axis=axis))], axis=axis)
    return later - field


def adjoint_shot(state, strains, shot_traces, shot_recv, lame_lambda, shear, buoyancy, solid_field):
    velocity = [state[0], state[1], state[2]]
    stress = [state[3 + k] for k in range(6)]
    grad_lam = jnp.zeros(lame_lambda.shape, jnp.float32)
    grad_shear = jnp.zeros(lame_lambda.shape, jnp.float32)
    shape = lame_lambda.shape
    for step in range(STEPS):
        velocity[0] = velocity[0] + COURANT * buoyancy * (back_diff(stress[0], 0) + back_diff(stress[3], 1) + back_diff(stress[4], 2))
        velocity[1] = velocity[1] + COURANT * buoyancy * (back_diff(stress[3], 0) + back_diff(stress[1], 1) + back_diff(stress[5], 2))
        velocity[2] = velocity[2] + COURANT * buoyancy * (back_diff(stress[4], 0) + back_diff(stress[5], 1) + back_diff(stress[2], 2))
        velocity[2] = velocity[2].reshape(-1).at[shot_recv].add(shot_traces[step]).reshape(shape)
        strain_xx = fore_diff(velocity[0], 0)
        strain_yy = fore_diff(velocity[1], 1)
        strain_zz = fore_diff(velocity[2], 2)
        shear_xy = fore_diff(velocity[0], 1) + fore_diff(velocity[1], 0)
        shear_xz = fore_diff(velocity[0], 2) + fore_diff(velocity[2], 0)
        shear_yz = fore_diff(velocity[1], 2) + fore_diff(velocity[2], 1)
        diverge = strain_xx + strain_yy + strain_zz
        stress[0] = stress[0] + COURANT * (lame_lambda * diverge + 2.0 * shear * strain_xx)
        stress[1] = stress[1] + COURANT * (lame_lambda * diverge + 2.0 * shear * strain_yy)
        stress[2] = stress[2] + COURANT * (lame_lambda * diverge + 2.0 * shear * strain_zz)
        stress[3] = stress[3] + COURANT * shear * shear_xy
        stress[4] = stress[4] + COURANT * shear * shear_xz
        stress[5] = stress[5] + COURANT * shear * shear_yz
        fwd = strains[step].astype(jnp.float32)
        grad_lam = grad_lam + diverge * (fwd[0] + fwd[1] + fwd[2])
        grad_shear = grad_shear + solid_field * (2.0 * (strain_xx * fwd[0] + strain_yy * fwd[1] + strain_zz * fwd[2]) + shear_xy * fwd[3] + shear_xz * fwd[4] + shear_yz * fwd[5])
    return jnp.stack(velocity + stress), grad_lam, grad_shear


def reference(adjoint_state, forward_strain, traces, receivers, sections, lame_lambda, lame_mu, buoyancy):
    solid_field = jnp.repeat(sections, CX).astype(jnp.float32)[:, None, None]
    shear = lame_mu * solid_field
    states = []
    total_lam = jnp.zeros(lame_lambda.shape, jnp.float32)
    total_mu = jnp.zeros(lame_lambda.shape, jnp.float32)
    for shot in range(SHOTS):
        final, grad_lam, grad_shear = adjoint_shot(adjoint_state[shot], forward_strain[shot], traces[shot], receivers[shot], lame_lambda, shear, buoyancy, solid_field)
        states.append(final)
        total_lam = total_lam + grad_lam
        total_mu = total_mu + grad_shear
    peak_lam = jnp.max(jnp.abs(total_lam))
    peak_mu = jnp.max(jnp.abs(total_mu))
    new_lam = lame_lambda * (1.0 - RATE * total_lam / (peak_lam + EPS))
    new_mu = lame_mu * (1.0 - RATE * total_mu / (peak_mu + EPS))
    return jnp.stack(states), jnp.stack([new_lam, new_mu])
```

```python
import jax
import jax.numpy as jnp
from jax import lax
from jax.sharding import PartitionSpec as P

STEPS = 4


COURANT = 0.15
RATE = 0.2
EPS = 1e-06


def shifted(block, axis, distance):
    devices = range(lax.axis_size(axis))
    route = [(i - distance, i) for i in devices if i - distance in devices]
    return lax.ppermute(block, axis, route)


def back_diff(field, axis):
    count = field.shape[axis]
    earlier = jnp.concatenate(
        [
            jnp.zeros_like(lax.slice_in_dim(field, 0, 1, axis=axis)),
            lax.slice_in_dim(field, 0, count - 1, axis=axis),
        ],
        axis=axis,
    )
    return field - earlier


def fore_diff(field, axis):
    count = field.shape[axis]
    later = jnp.concatenate(
        [
            lax.slice_in_dim(field, 1, count, axis=axis),
            jnp.zeros_like(lax.slice_in_dim(field, 0, 1, axis=axis)),
        ],
        axis=axis,
    )
    return later - field


def back_plane(field, plane):
    return field - jnp.concatenate([plane[None], field[:-1]], axis=0)


def fore_plane(field, plane):
    return jnp.concatenate([field[1:], plane[None]], axis=0) - field


def shards(
    adjoint_state, forward_strain, traces, receivers, sections, lame_lambda, lame_mu, buoyancy
):
    state = adjoint_state[0]
    strains = forward_strain[0]
    shot_traces = traces[0]
    shot_recv = receivers[0]
    shape = lame_lambda.shape
    cells = shape[0] * shape[1] * shape[2]
    slab = lax.axis_index("space")
    solid_flag = lax.dynamic_index_in_dim(sections, slab, keepdims=False)
    solid = solid_flag.astype(jnp.float32)
    shear = lame_mu * solid
    local = shot_recv - slab * cells
    rows = shape[0] * shape[1]
    row_hot = (lax.broadcasted_iota(jnp.int32, (rows, 256), 0) == (local >> 8)[None, :]).astype(jnp.float32)
    lane_hot = (lax.broadcasted_iota(jnp.int32, (256, shape[2]), 1) == (local & 255)[:, None]).astype(jnp.float32)
    velocity = [state[0], state[1], state[2]]
    stress = [state[3 + k] for k in range(6)]
    grad_lam = jnp.zeros(shape, jnp.float32)
    grad_shear = jnp.zeros(shape, jnp.float32)
    zero = jnp.zeros(shape[1:], jnp.float32)
    factor = COURANT * buoyancy
    factor_right = None
    for step in range(STEPS):
        amount = jnp.dot(row_hot, lane_hot * shot_traces[step][:, None], precision=lax.Precision.HIGHEST)
        part = [
            velocity[0] + factor * (back_plane(stress[0], zero) + back_diff(stress[3], 1) + back_diff(stress[4], 2)),
            velocity[1] + factor * (back_plane(stress[3], zero) + back_diff(stress[1], 1) + back_diff(stress[5], 2)),
            velocity[2] + factor * (back_plane(stress[4], zero) + back_diff(stress[5], 1) + back_diff(stress[2], 2))
            + amount.reshape(shape),
        ]
        last = [stress[0][-1], stress[3][-1], stress[4][-1]]
        left = shifted(jnp.stack(last), "space", 1)
        firsts = [p[0] for p in part]
        if step == 0:
            firsts = firsts + [factor[0]]
        right = shifted(jnp.stack(firsts), "space", -1)
        if step == 0:
            factor_right = right[3]
        velocity = [
            jnp.concatenate([(part[k][0] - factor[0] * left[k])[None], part[k][1:]], axis=0) for k in range(3)
        ]
        beyond = [right[k] - factor_right * last[k] for k in range(3)]
        fwd = strains[step].astype(jnp.float32)
        exx = fore_plane(velocity[0], beyond[0])
        eyy = fore_diff(velocity[1], 1)
        ezz = fore_diff(velocity[2], 2)
        gxy = fore_diff(velocity[0], 1) + fore_plane(velocity[1], beyond[1])
        gxz = fore_diff(velocity[0], 2) + fore_plane(velocity[2], beyond[2])
        gyz = fore_diff(velocity[1], 2) + fore_diff(velocity[2], 1)
        div = exx + eyy + ezz
        stress = [
            stress[0] + COURANT * (lame_lambda * div + 2.0 * shear * exx),
            stress[1] + COURANT * (lame_lambda * div + 2.0 * shear * eyy),
            stress[2] + COURANT * (lame_lambda * div + 2.0 * shear * ezz),
            stress[3] + COURANT * shear * gxy,
            stress[4] + COURANT * shear * gxz,
            stress[5] + COURANT * shear * gyz,
        ]
        grad_lam = grad_lam + div * (fwd[0] + fwd[1] + fwd[2])
        grad_shear = grad_shear + solid * (
            2.0 * (exx * fwd[0] + eyy * fwd[1] + ezz * fwd[2]) + gxy * fwd[3] + gxz * fwd[4] + gyz * fwd[5]
        )
    final_state = jnp.stack(velocity + stress)[None]
    return (final_state, updated_model(grad_lam, grad_shear, lame_lambda, lame_mu))


def updated_model(grad_lam, grad_shear, lame_lambda, lame_mu):
    partner = [(0, 1), (1, 0), (2, 3), (3, 2)]
    across = [(0, 2), (2, 0), (1, 3), (3, 1)]
    even = lax.axis_index("shot") % 2 == 0
    keep = jnp.where(even, grad_lam, grad_shear)
    give = jnp.where(even, grad_shear, grad_lam)
    half = keep + lax.ppermute(give, "shot", partner)
    total = half + lax.ppermute(half, "shot", across)
    other = lax.ppermute(total, "shot", partner)
    peak = jnp.max(jnp.abs(total))
    pair = jnp.stack([jnp.where(even, peak, 0.0), jnp.where(even, 0.0, peak)])
    peaks = lax.pmax(pair, ("space", "shot"))
    total_lam = jnp.where(even, total, other)
    total_mu = jnp.where(even, other, total)
    return jnp.stack(
        [
            lame_lambda * (1.0 - RATE * total_lam / (peaks[0] + EPS)),
            lame_mu * (1.0 - RATE * total_mu / (peaks[1] + EPS)),
        ]
    )


def solution(mesh):
    return jax.shard_map(
        shards,
        mesh=mesh,
        in_specs=(
            P("shot", None, "space", None, None),
            P("shot", None, None, "space", None, None),
            P("shot", None, None),
            P("shot", None),
            P(),
            P("space", None, None),
            P("space", None, None),
            P("space", None, None),
        ),
        out_specs=(P("shot", None, "space", None, None), P(None, "space", None, None)),
        check_vma=False,
    )
```

```python
import jax
import jax.numpy as jnp
from jax import lax
from jax.sharding import PartitionSpec as P

STEPS = 4


COURANT = 0.15
RATE = 0.2
EPS = 1e-06


def shifted(block, axis, distance):
    devices = range(lax.axis_size(axis))
    route = [(i - distance, i) for i in devices if i - distance in devices]
    return lax.ppermute(block, axis, route)


def back_diff(field, axis):
    count = field.shape[axis]
    earlier = jnp.concatenate(
        [
            jnp.zeros_like(lax.slice_in_dim(field, 0, 1, axis=axis)),
            lax.slice_in_dim(field, 0, count - 1, axis=axis),
        ],
        axis=axis,
    )
    return field - earlier


def fore_diff(field, axis):
    count = field.shape[axis]
    later = jnp.concatenate(
        [
            lax.slice_in_dim(field, 1, count, axis=axis),
            jnp.zeros_like(lax.slice_in_dim(field, 0, 1, axis=axis)),
        ],
        axis=axis,
    )
    return later - field


def back_plane(field, plane):
    return field - jnp.concatenate([plane[None], field[:-1]], axis=0)


def fore_plane(field, plane):
    return jnp.concatenate([field[1:], plane[None]], axis=0) - field


def shards(
    adjoint_state, forward_strain, traces, receivers, sections, lame_lambda, lame_mu, buoyancy
):
    state = adjoint_state[0]
    strains = forward_strain[0]
    shot_traces = traces[0]
    shot_recv = receivers[0]
    shape = lame_lambda.shape
    cells = shape[0] * shape[1] * shape[2]
    slab = lax.axis_index("space")
    solid_flag = lax.dynamic_index_in_dim(sections, slab, keepdims=False)
    solid = solid_flag.astype(jnp.float32)
    shear = lame_mu * solid
    local = shot_recv - slab * cells
    rows = shape[0] * shape[1]
    row_hot = (lax.broadcasted_iota(jnp.int32, (rows, 256), 0) == (local >> 8)[None, :]).astype(jnp.float32)
    lane_hot = (lax.broadcasted_iota(jnp.int32, (256, shape[2]), 1) == (local & 255)[:, None]).astype(jnp.float32)
    velocity = [state[0], state[1], state[2]]
    stress = [state[3 + k] for k in range(6)]
    grad_lam = jnp.zeros(shape, jnp.float32)
    grad_shear = jnp.zeros(shape, jnp.float32)
    zero = jnp.zeros(shape[1:], jnp.float32)
    factor = COURANT * buoyancy
    factor_right = None
    for step in range(STEPS):
        amount = jnp.dot(row_hot, lane_hot * shot_traces[step][:, None], precision=lax.Precision.HIGHEST)
        part = [
            velocity[0] + factor * (back_plane(stress[0], zero) + back_diff(stress[3], 1) + back_diff(stress[4], 2)),
            velocity[1] + factor * (back_plane(stress[3], zero) + back_diff(stress[1], 1) + back_diff(stress[5], 2)),
            velocity[2] + factor * (back_plane(stress[4], zero) + back_diff(stress[5], 1) + back_diff(stress[2], 2))
            + amount.reshape(shape),
        ]
        last = [stress[0][-1], stress[3][-1], stress[4][-1]]
        left = shifted(jnp.stack(last), "space", 1)
        firsts = [p[0] for p in part]
        if step == 0:
            firsts = firsts + [factor[0]]
        right = shifted(jnp.stack(firsts), "space", -1)
        if step == 0:
            factor_right = right[3]
        velocity = [
            jnp.concatenate([(part[k][0] - factor[0] * left[k])[None], part[k][1:]], axis=0) for k in range(3)
        ]
        beyond = [right[k] - factor_right * last[k] for k in range(3)]
        fwd = strains[step].astype(jnp.float32)
        exx = fore_plane(velocity[0], beyond[0])
        eyy = fore_diff(velocity[1], 1)
        ezz = fore_diff(velocity[2], 2)
        gxy = fore_diff(velocity[0], 1) + fore_plane(velocity[1], beyond[1])
        gxz = fore_diff(velocity[0], 2) + fore_plane(velocity[2], beyond[2])
        gyz = fore_diff(velocity[1], 2) + fore_diff(velocity[2], 1)
        div = exx + eyy + ezz
        stress = [
            stress[0] + COURANT * (lame_lambda * div + 2.0 * shear * exx),
            stress[1] + COURANT * (lame_lambda * div + 2.0 * shear * eyy),
            stress[2] + COURANT * (lame_lambda * div + 2.0 * shear * ezz),
            stress[3] + COURANT * shear * gxy,
            stress[4] + COURANT * shear * gxz,
            stress[5] + COURANT * shear * gyz,
        ]
        grad_lam = grad_lam + div * (fwd[0] + fwd[1] + fwd[2])
        grad_shear = grad_shear + solid * (
            2.0 * (exx * fwd[0] + eyy * fwd[1] + ezz * fwd[2]) + gxy * fwd[3] + gxz * fwd[4] + gyz * fwd[5]
        )
    final_state = jnp.stack(velocity + stress)[None]
    return (final_state, updated_model(grad_lam, grad_shear, lame_lambda, lame_mu))


def space_peak(value):
    count = lax.axis_size("space")
    for stride, size in ((2, 4), (8, 4), (1, 2)):
        span = stride * size
        arrived = []
        for turn in range(1, size):
            route = [(i, i // span * span + (i + turn * stride) % span) for i in range(count)]
            arrived.append(lax.ppermute(value, "space", route))
        for item in arrived:
            value = jnp.maximum(value, item)
    return value


def updated_model(grad_lam, grad_shear, lame_lambda, lame_mu):
    partner = [(0, 1), (1, 0), (2, 3), (3, 2)]
    across = [(0, 2), (2, 0), (1, 3), (3, 1)]
    even = lax.axis_index("shot") % 2 == 0
    keep = jnp.where(even, grad_lam, grad_shear)
    give = jnp.where(even, grad_shear, grad_lam)
    half = keep + lax.ppermute(give, "shot", partner)
    total = half + lax.ppermute(half, "shot", across)
    other = lax.ppermute(total, "shot", partner)
    peak = jnp.max(jnp.abs(total))
    own = space_peak(jnp.full((8, 128), peak))
    theirs = lax.ppermute(own, "shot", partner)
    peaks = (jnp.where(even, own, theirs)[0, 0], jnp.where(even, theirs, own)[0, 0])
    total_lam = jnp.where(even, total, other)
    total_mu = jnp.where(even, other, total)
    return jnp.stack(
        [
            lame_lambda * (1.0 - RATE * total_lam / (peaks[0] + EPS)),
            lame_mu * (1.0 - RATE * total_mu / (peaks[1] + EPS)),
        ]
    )


def solution(mesh):
    return jax.shard_map(
        shards,
        mesh=mesh,
        in_specs=(
            P("shot", None, "space", None, None),
            P("shot", None, None, "space", None, None),
            P("shot", None, None),
            P("shot", None),
            P(),
            P("space", None, None),
            P("space", None, None),
            P("space", None, None),
        ),
        out_specs=(P("shot", None, "space", None, None), P(None, "space", None, None)),
        check_vma=False,
    )
```

```python
import jax
import jax.numpy as jnp
from jax import lax
from jax.sharding import PartitionSpec as P

STEPS = 4


COURANT = 0.15
RATE = 0.2
EPS = 1e-06


def shifted(block, axis, distance):
    devices = range(lax.axis_size(axis))
    route = [(i - distance, i) for i in devices if i - distance in devices]
    return lax.ppermute(block, axis, route)


def back_diff(field, axis):
    count = field.shape[axis]
    earlier = jnp.concatenate(
        [
            jnp.zeros_like(lax.slice_in_dim(field, 0, 1, axis=axis)),
            lax.slice_in_dim(field, 0, count - 1, axis=axis),
        ],
        axis=axis,
    )
    return field - earlier


def fore_diff(field, axis):
    count = field.shape[axis]
    later = jnp.concatenate(
        [
            lax.slice_in_dim(field, 1, count, axis=axis),
            jnp.zeros_like(lax.slice_in_dim(field, 0, 1, axis=axis)),
        ],
        axis=axis,
    )
    return later - field


def back_plane(field, plane):
    return field - jnp.concatenate([plane[None], field[:-1]], axis=0)


def fore_plane(field, plane):
    return jnp.concatenate([field[1:], plane[None]], axis=0) - field


def shards(
    adjoint_state, forward_strain, traces, receivers, sections, lame_lambda, lame_mu, buoyancy
):
    state = adjoint_state[0]
    strains = forward_strain[0]
    shot_traces = traces[0]
    shot_recv = receivers[0]
    shape = lame_lambda.shape
    cells = shape[0] * shape[1] * shape[2]
    slab = lax.axis_index("space")
    solid_flag = lax.dynamic_index_in_dim(sections, slab, keepdims=False)
    solid = solid_flag.astype(jnp.float32)
    shear = lame_mu * solid
    local = shot_recv - slab * cells
    rows = shape[0] * shape[1]
    row_hot = (lax.broadcasted_iota(jnp.int32, (rows, 256), 0) == (local >> 8)[None, :]).astype(jnp.float32)
    lane_hot = (lax.broadcasted_iota(jnp.int32, (256, shape[2]), 1) == (local & 255)[:, None]).astype(jnp.float32)
    velocity = [state[0], state[1], state[2]]
    stress = [state[3 + k] for k in range(6)]
    grad_lam = jnp.zeros(shape, jnp.float32)
    grad_shear = jnp.zeros(shape, jnp.float32)
    zero = jnp.zeros(shape[1:], jnp.float32)
    factor = COURANT * buoyancy
    factor_right = None
    for step in range(STEPS):
        amount = jnp.dot(row_hot, lane_hot * shot_traces[step][:, None], precision=lax.Precision.HIGHEST)
        part = [
            velocity[0] + factor * (back_plane(stress[0], zero) + back_diff(stress[3], 1) + back_diff(stress[4], 2)),
            velocity[1] + factor * (back_plane(stress[3], zero) + back_diff(stress[1], 1) + back_diff(stress[5], 2)),
            velocity[2] + factor * (back_plane(stress[4], zero) + back_diff(stress[5], 1) + back_diff(stress[2], 2))
            + amount.reshape(shape),
        ]
        last = [stress[0][-1], stress[3][-1], stress[4][-1]]
        firsts = [p[0] for p in part]
        if step == 0:
            firsts = firsts + [factor[0]]
        ahead, behind = lax.optimization_barrier((jnp.stack(last), jnp.stack(firsts)))
        right = shifted(behind, "space", -1)
        left = shifted(ahead, "space", 1)
        if step == 0:
            factor_right = right[3]
        velocity = [
            jnp.concatenate([(part[k][0] - factor[0] * left[k])[None], part[k][1:]], axis=0) for k in range(3)
        ]
        beyond = [right[k] - factor_right * last[k] for k in range(3)]
        fwd = strains[step].astype(jnp.float32)
        exx = fore_plane(velocity[0], beyond[0])
        eyy = fore_diff(velocity[1], 1)
        ezz = fore_diff(velocity[2], 2)
        gxy = fore_diff(velocity[0], 1) + fore_plane(velocity[1], beyond[1])
        gxz = fore_diff(velocity[0], 2) + fore_plane(velocity[2], beyond[2])
        gyz = fore_diff(velocity[1], 2) + fore_diff(velocity[2], 1)
        div = exx + eyy + ezz
        stress = [
            stress[0] + COURANT * (lame_lambda * div + 2.0 * shear * exx),
            stress[1] + COURANT * (lame_lambda * div + 2.0 * shear * eyy),
            stress[2] + COURANT * (lame_lambda * div + 2.0 * shear * ezz),
            stress[3] + COURANT * shear * gxy,
            stress[4] + COURANT * shear * gxz,
            stress[5] + COURANT * shear * gyz,
        ]
        grad_lam = grad_lam + div * (fwd[0] + fwd[1] + fwd[2])
        grad_shear = grad_shear + solid * (
            2.0 * (exx * fwd[0] + eyy * fwd[1] + ezz * fwd[2]) + gxy * fwd[3] + gxz * fwd[4] + gyz * fwd[5]
        )
        if step < STEPS - 1:
            grad_lam, grad_shear = lax.optimization_barrier((grad_lam, grad_shear))
    final_state = jnp.stack(velocity + stress)[None]
    return (final_state, updated_model(grad_lam, grad_shear, lame_lambda, lame_mu))


def space_peak(value):
    count = lax.axis_size("space")
    for stride, size in ((2, 4), (8, 4), (1, 2)):
        span = stride * size
        arrived = []
        for turn in range(1, size):
            route = [(i, i // span * span + (i + turn * stride) % span) for i in range(count)]
            arrived.append(lax.ppermute(value, "space", route))
        for item in arrived:
            value = jnp.maximum(value, item)
    return value


def updated_model(grad_lam, grad_shear, lame_lambda, lame_mu):
    partner = [(0, 1), (1, 0), (2, 3), (3, 2)]
    across = [(0, 2), (2, 0), (1, 3), (3, 1)]
    even = lax.axis_index("shot") % 2 == 0
    keep = jnp.where(even, grad_lam, grad_shear)
    give = jnp.where(even, grad_shear, grad_lam)
    half = keep + lax.ppermute(give, "shot", partner)
    total = half + lax.ppermute(half, "shot", across)
    other = lax.ppermute(total, "shot", partner)
    peak = jnp.max(jnp.abs(total))
    own = space_peak(jnp.full((8, 128), peak))
    theirs = lax.ppermute(own, "shot", partner)
    peaks = (jnp.where(even, own, theirs)[0, 0], jnp.where(even, theirs, own)[0, 0])
    total_lam = jnp.where(even, total, other)
    total_mu = jnp.where(even, other, total)
    return jnp.stack(
        [
            lame_lambda * (1.0 - RATE * total_lam / (peaks[0] + EPS)),
            lame_mu * (1.0 - RATE * total_mu / (peaks[1] + EPS)),
        ]
    )


def solution(mesh):
    return jax.shard_map(
        shards,
        mesh=mesh,
        in_specs=(
            P("shot", None, "space", None, None),
            P("shot", None, None, "space", None, None),
            P("shot", None, None),
            P("shot", None),
            P(),
            P("space", None, None),
            P("space", None, None),
            P("space", None, None),
        ),
        out_specs=(P("shot", None, "space", None, None), P(None, "space", None, None)),
        check_vma=False,
    )
```
